32 devices in a mesh: tm: 4 (over y, core), space: 8 (over z, x).
Axes of the slice: x: 2, y: 2, z: 4, core: 2. Of those that a mesh axis runs over, the one named last changes fastest.
Arguments:
- base: float32 [2, 4, 16, 64, 128], P(None, 'tm', 'space'), may hold values from -6 to 6
- phi_prev: float32 [4, 16, 64, 128], P('tm', 'space'), may hold values from -6 to 6
- masks: int32 [2, 16, 64, 128], P(None, 'space'), may hold values from 0 to 1, as said below
- enc_w: bfloat16 [16, 1, 3, 3, 3], replicated, may hold values from -1.25 to 1.25
- enc_b: float32 [16], replicated, may hold values from -0.5 to 0.5
- in_w: bfloat16 [2, 16, 1, 3, 3, 3], replicated, may hold values from -1.25 to 1.25
- ctx_w: bfloat16 [2, 16, 16], replicated, may hold values from -1.5 to 1.5
- hid_b: float32 [2, 16], replicated, may hold values from -0.5 to 0.5
- mid_w: bfloat16 [2, 16, 16, 3, 3, 3], replicated, may hold values from -0.3125 to 0.3125
- mid_b: float32 [2, 16], replicated, may hold values from -0.5 to 0.5
- out_w: bfloat16 [2, 2, 16], replicated, may hold values from -1.5 to 1.5
- out_b: float32 [2, 2], replicated, may hold values from -0.5 to 0.5
Outputs:
- samples: float32 [2, 4, 16, 64, 128], P(None, 'tm', 'space')
- logdet: float32 [2, 4], P(None, 'tm')
The draws below stay inside these ranges and needn't reach their ends.
Inputs may be any that keep to these rules, and one draw needn't show every extreme that they name: `masks`: each layer's mask is a checkerboard of 0 and 1 in the three lattice coordinates, its parity chosen per layer.
All inputs are finite; a program needn't handle non-finite values.
Results may differ from the reference program's by a relative error of at most 0.0043.
Values may be sent and summed in bfloat16 or wider, within the bound.
No kernel may reach another device: no remote copies, remote signals or barrier semaphores. Data moves between devices by JAX's collectives and lax.ppermute only.
A program may use at most 128 MiB of HBM per device.

```python
import jax
import jax.numpy as jnp
from jax import lax

CH = 16
LAYERS = 2
TICKS = 2
LY = 64
LZ = 128
NX = 16
NT = 4


def draw_masks(key, part):
    parity = jax.random.randint(key, (LAYERS, 1, 1, 1), 0, 2)
    shape = (LAYERS, NX, LY, LZ)
    coords = lax.broadcasted_iota(jnp.int32, shape, 1) + lax.broadcasted_iota(jnp.int32, shape, 2) + lax.broadcasted_iota(jnp.int32, shape, 3)
    return ((coords + parity) % 2).astype(jnp.int32)


def levels(stream_key, shape, pieces, smallest, largest):
    def one(dim, parts):
        draws = jax.random.uniform(jax.random.fold_in(jax.random.fold_in(stream_key, 6), dim), (parts,), jnp.float32, smallest / len(pieces), largest / len(pieces))
        return jnp.repeat(jnp.exp(draws), shape[dim] // parts).reshape((-1,) + (1,) * (len(shape) - dim - 1))

    factor_of = one(*pieces[0])
    for cut in pieces[1:]:
        factor_of = factor_of * one(*cut)
    return factor_of


def bell_draw(rng, extent, width, bound, cuts=(), dtype=jnp.bfloat16):
    array = width * jax.random.normal(rng, extent, jnp.float32)
    if cuts:
        array = array * levels(rng, extent, cuts, -0.22, 0.18)
    return jnp.clip(array, -bound, bound).astype(dtype)


def setup_inputs(seed: int = 0) -> dict:
    key_of = jax.random.split(jax.random.key(seed), 13)
    return {
        "base": bell_draw(key_of[0], (TICKS, NT, NX, LY, LZ), 1.0, 6.0, ((1, 4), (2, 8)), jnp.float32),
        "phi_prev": bell_draw(key_of[1], (NT, NX, LY, LZ), 1.0, 6.0, ((0, 4), (1, 8)), jnp.float32),
        "masks": draw_masks(jax.random.fold_in(key_of[12], 71), 0),
        "enc_w": bell_draw(key_of[3], (CH, 1, 3, 3, 3), 27 ** -0.5, 1.25),
        "enc_b": jnp.clip(jax.random.uniform(key_of[4], (CH,), jnp.float32, -0.5, 0.5), -0.5, 0.5),
        "in_w": bell_draw(key_of[5], (LAYERS, CH, 1, 3, 3, 3), 27 ** -0.5, 1.25),
        "ctx_w": bell_draw(key_of[6], (LAYERS, CH, CH), CH ** -0.5, 1.5),
        "hid_b": jnp.clip(jax.random.uniform(key_of[7], (LAYERS, CH), jnp.float32, -0.5, 0.5), -0.5, 0.5),
        "mid_w": bell_draw(key_of[8], (LAYERS, CH, CH, 3, 3, 3), (27 * CH) ** -0.5, 0.3125),
        "mid_b": jnp.clip(jax.random.uniform(key_of[9], (LAYERS, CH), jnp.float32, -0.5, 0.5), -0.5, 0.5),
        "out_w": bell_draw(key_of[10], (LAYERS, 2, CH), CH ** -0.5, 1.5),
        "out_b": jnp.clip(jax.random.uniform(key_of[11], (LAYERS, 2), jnp.float32, -0.5, 0.5), -0.5, 0.5),
    }


def conv_wrap(v, w, widths):
    padded = jnp.pad(v, widths, mode="wrap")
    return lax.conv_general_dilated(padded[None], w, (1, 1, 1), "VALID", dimension_numbers=("NCDHW", "OIDHW", "NCDHW"), preferred_element_type=jnp.float32)[0]


def encode(slice_field, enc_w, enc_b):
    widths = ((0, 0), (1, 1), (1, 1), (1, 1))
    value = conv_wrap(slice_field.astype(jnp.bfloat16)[None], enc_w, widths)
    return jnp.tanh(value + enc_b[:, None, None, None]).astype(jnp.bfloat16)


def couple(start, context, masks, in_w, ctx_w, hid_b, mid_w, mid_b, out_w, out_b):
    widths = ((0, 0), (1, 1), (1, 1), (1, 1))
    phi = start
    total = jnp.zeros((), jnp.float32)
    for layer in range(LAYERS):
        keep = masks[layer].astype(jnp.float32)
        frozen = (keep * phi).astype(jnp.bfloat16)[None]
        mixed = jnp.einsum("oc,cxyz->oxyz", ctx_w[layer].astype(jnp.float32), context.astype(jnp.float32))
        first = conv_wrap(frozen, in_w[layer], widths) + mixed + hid_b[layer][:, None, None, None]
        hidden = jnp.tanh(first).astype(jnp.bfloat16)
        second = conv_wrap(hidden, mid_w[layer], widths) + mid_b[layer][:, None, None, None]
        deeper = jnp.tanh(second).astype(jnp.bfloat16)
        output = jnp.einsum("oc,cxyz->oxyz", out_w[layer].astype(jnp.float32), deeper.astype(jnp.float32)) + out_b[layer][:, None, None, None]
        scale = jnp.tanh(output[0])
        phi = keep * phi + (1.0 - keep) * (phi * jnp.exp(scale) + output[1])
        total = total + jnp.sum((1.0 - keep) * scale)
    return phi, total


def reference(base, phi_prev, masks, enc_w, enc_b, in_w, ctx_w, hid_b, mid_w, mid_b, out_w, out_b):
    previous = phi_prev
    samples = []
    logdets = []
    for tick in range(TICKS):
        shifted = jnp.roll(previous, 1, axis=0)

        def one_slice(pair):
            start, earlier = pair
            context = encode(earlier, enc_w, enc_b)
            return couple(start, context, masks, in_w, ctx_w, hid_b, mid_w, mid_b, out_w, out_b)

        phi, total = lax.map(one_slice, (base[tick], shifted))
        samples.append(phi)
        logdets.append(total / (NX * LY * LZ))
        previous = phi
    return jnp.stack(samples), jnp.stack(logdets)
```

```python
import functools

import jax
import jax.numpy as jnp
from jax import lax
from jax.experimental import pallas as pl
from jax.experimental.pallas import tpu as pltpu
from jax.sharding import PartitionSpec as P

LAYERS = 2
TICKS = 2
CH = 16
BF = jnp.bfloat16
F32 = jnp.float32

PX = 2
HALO = 4
FX = PX + 2 * HALO
HX0 = FX - 2
GR = 32
BY = 4


def one_hot(shape, fn):
    row = lax.broadcasted_iota(jnp.int32, shape, 0)
    col = lax.broadcasted_iota(jnp.int32, shape, 1)
    return jnp.where(fn(row, col), 1.0, 0.0).astype(BF)


def exact_dot(a, b):
    return jnp.dot(a, b, preferred_element_type=F32)


def col_dot(a, b):
    return lax.dot_general(a, b, (((0,), (0,)), ((), ())), preferred_element_type=F32)


def split2(value):
    high = value.astype(BF)
    low = (value - high.astype(F32)).astype(BF)
    return jnp.concatenate([high, low], axis=0)


def prep_kernel(enc_ref, enc_b_ref, in_ref, hid_b_ref, ctx_ref, mid_ref, mid_b_ref, out_ref,
                wenc_ref, win0_ref, win1_ref, wctx_ref, wmid_ref, bmid_ref, wout_ref):
    lanes = 2 * 128

    def taps(load):
        return jnp.concatenate([load(k) for k in range(9)], axis=0)

    def banded(rows27, bias2, planes, shift0, dst):
        def place(row, col):
            dx, dy, dz = row // 9, (row // 3) % 3, row % 3
            return col == dy * GR + dz * FX + dx
        base = col_dot(rows27, one_hot((27, lanes), place))
        extra = col_dot(bias2, one_hot((2, lanes), lambda row, col: col == 3 * FX + row))
        for y in range(BY):
            for x in range(planes):
                shift = y * GR + x + shift0
                moved = base if shift == 0 else pltpu.roll(base, shift, 1)
                r = (y * planes + x) * CH
                dst[r:r + CH, :] = (moved + extra).astype(BF)

    banded(taps(lambda k: enc_ref[k].astype(F32)).astype(BF), split2(enc_b_ref[...]), HX0, 0, wenc_ref)
    for layer, (dst, planes, shift0) in enumerate(((win0_ref, HX0, 0), (win1_ref, HX0 - 4, 2))):
        rows = taps(lambda k: in_ref[k, :, layer, :].astype(F32)).astype(BF)
        banded(rows, split2(hid_b_ref[layer:layer + 1, :]), planes, shift0, dst)

    spread = one_hot((CH, 256), lambda row, col: col % CH == row)
    row = lax.broadcasted_iota(jnp.int32, (256, 256), 0)
    col = lax.broadcasted_iota(jnp.int32, (256, 256), 1)
    for layer in range(LAYERS):
        wide = exact_dot(ctx_ref[layer], spread)
        tall = jnp.concatenate([wide] * 16, axis=0)
        wctx_ref[layer] = jnp.where(row // CH == col // CH, tall, 0.0).astype(BF)
        narrow = exact_dot(out_ref[layer], spread)
        for o in range(2):
            line = jnp.broadcast_to(narrow[o:o + 1, :], (16, 256))
            r = row[:16] % 8 * 2 + row[:16] // 8
            wout_ref[layer, o * 16:o * 16 + 16, :] = jnp.where(col[:16] // CH == r, line, 0.0).astype(BF)
        bias2 = split2(mid_b_ref[layer:layer + 1, :])
        bmid_ref[layer] = col_dot(bias2, jnp.ones((2, 128), BF))
        zero = jnp.zeros((CH, CH), F32)
        for dz in range(3):
            pieces = []
            for dy in range(3):
                for dx in range(3):
                    pieces.append(mid_ref[layer, (dx * 3 + dy) * 3 + dz].astype(F32))
                pieces.append(zero)
            base = jnp.concatenate(pieces + [zero] * 12, axis=1)
            for y in range(BY):
                for x in range(2):
                    shift = (y * 4 + x) * CH
                    moved = base if shift == 0 else pltpu.roll(base, shift, 1)
                    r = (y * 2 + x) * CH
                    wmid_ref[layer, r:r + CH, dz * 384:dz * 384 + 384] = moved.astype(BF)


def tick_kernel(tick, lines, prev_refs, base_refs, mask_ref, wenc_ref, win0_ref, win1_ref, wctx_ref,
                wmid_ref, bmid_ref, wout_ref, out_b_ref, phi_ref, send_ref, sum_ref, g_ref, gb_ref, c_ref,
                h_ref, keep_ref):
    steps = lines // (2 * BY)
    nz = 128

    def gather_plane(p, first, value):
        rows = value.shape[0]
        for dz in range(3):
            moved = value if dz == 1 else pltpu.roll(value, 1 if dz == 0 else nz - 1, 1)
            g_ref[pl.ds(first * GR + dz * FX + p, rows, stride=GR), :] = moved

    def gather_done():
        for line in range(lines):
            gb_ref[(line + 1) * GR:(line + 2) * GR, :] = g_ref[line * GR:(line + 1) * GR, :].astype(BF)
        gb_ref[0:GR, :] = gb_ref[lines * GR:(lines + 1) * GR, :]
        gb_ref[(lines + 1) * GR:(lines + 2) * GR, :] = gb_ref[GR:2 * GR, :]

    def window(y0):
        left = gb_ref[y0 * GR:(y0 + BY + 2) * GR, :]
        right = gb_ref[(y0 + BY) * GR:(y0 + 2 * BY + 2) * GR, :]
        return jnp.concatenate([left, right], axis=1)

    def store_hidden(y, value, size):
        count = value.shape[0] // size
        for dz in range(3):
            moved = value if dz == 1 else pltpu.roll(value, 1 if dz == 0 else nz - 1, 1)
            h_ref[dz, y + 1:y + 1 + count, 0:size, :] = moved.astype(BF).reshape(count, size, nz)

    def wrap_hidden(size):
        for dz in range(3):
            h_ref[dz, 0, 0:size, :] = h_ref[dz, lines, 0:size, :]
            h_ref[dz, lines + 1, 0:size, :] = h_ref[dz, 1, 0:size, :]

    kin = (BY + 2) * GR

    ones = jnp.ones((lines, nz), F32)
    for k in range(2):
        g_ref[pl.ds(3 * FX + k, lines, stride=GR), :] = ones

    for k, ref in enumerate(prev_refs):
        for j in range(PX):
            gather_plane(k * PX + j, 0, ref[j].astype(F32))
    gather_done()
    size = HX0 * CH
    for i in range(steps):
        y0 = i * 2 * BY
        rhs = window(y0)
        for part in range(2):
            w = wenc_ref[part * 256:part * 256 + 256, 0:kin]
            value = jnp.tanh(exact_dot(w, rhs)).astype(BF)
            for half in range(2):
                y = y0 + half * BY + part * 2
                c_ref[y:y + 2] = value[:, half * nz:half * nz + nz].reshape(2, size, nz)

    def start_plane(p, layer):
        k, j = divmod(p, PX)
        ref = base_refs[k]
        return ref[tick, j].astype(F32)

    for p in range(FX):
        gather_plane(p, 0, mask_ref[0, p % PX].astype(F32) * start_plane(p, 0))
    gather_done()
    for i in range(steps):
        y0 = i * 2 * BY
        rhs = window(y0)
        for part in range(2):
            y = y0 + part * 2
            ctx = jnp.concatenate(
                [c_ref[y:y + 2].reshape(256, nz), c_ref[y + BY:y + BY + 2].reshape(256, nz)], axis=1
            )
            first = exact_dot(win0_ref[part * 256:part * 256 + 256, 0:kin], rhs) + exact_dot(wctx_ref[0], ctx)
            value = jnp.tanh(first)
            for half in range(2):
                store_hidden(y + half * BY, value[:, half * nz:half * nz + nz], size)
    wrap_hidden(size)

    def middle(layer, y0, x0):
        parts = []
        for dz in range(3):
            side = []
            for half in range(2):
                y = y0 + half * BY
                block = h_ref[dz, y:y + BY + 2, x0 * CH:(x0 + 4) * CH, :]
                side.append(block.reshape((BY + 2) * 4 * CH, nz))
            parts.append(jnp.concatenate(side, axis=1))
        second = exact_dot(wmid_ref[layer], jnp.concatenate(parts, axis=0))
        bias = jnp.concatenate([bmid_ref[layer]] * 8, axis=0)
        second = second + jnp.concatenate([bias, bias], axis=1)
        deeper = jnp.tanh(second).astype(BF)
        return jnp.concatenate([deeper[:, :nz], deeper[:, nz:]], axis=0)

    def couple(layer, keep, phi, o0, o1):
        scale = jnp.tanh(o0 + out_b_ref[layer, 0])
        drop = 1.0 - keep
        moved = keep * phi + drop * (phi * jnp.exp(scale) + (o1 + out_b_ref[layer, 1]))
        return moved, drop * scale

    total = jnp.zeros((8, nz), F32)
    for i in range(steps):
        y0 = i * 2 * BY
        rows = slice(y0, y0 + 2 * BY)
        deep = jnp.concatenate([middle(0, y0, x0) for x0 in (0, 2, 4)], axis=1)
        o = exact_dot(wout_ref[0], deep)
        for j in range(6):
            p = j + 2
            k, jj = divmod(p, PX)
            lane = slice((j // 2) * nz, (j // 2) * nz + nz)
            r = (j % 2) * 8
            keep = mask_ref[0, p % PX, rows, :].astype(F32)
            phi = base_refs[k][tick, jj, rows, :].astype(F32)
            phi, part = couple(0, keep, phi, o[r:r + 8, lane], o[16 + r:24 + r, lane])
            if k == 2:
                keep_ref[jj, rows, :] = phi
                total = total + part
            gather_plane(p, y0, mask_ref[1, p % PX, rows, :].astype(F32) * phi)

    gather_done()
    size1 = (HX0 - 4) * CH
    for i in range(steps):
        y0 = i * 2 * BY
        ctx = jnp.concatenate(
            [c_ref[y:y + BY, 2 * CH:6 * CH, :].reshape(256, nz) for y in (y0, y0 + BY)], axis=1
        )
        first = exact_dot(win1_ref[:, 0:kin], window(y0)) + exact_dot(wctx_ref[1], ctx)
        value = jnp.tanh(first)
        for half in range(2):
            store_hidden(y0 + half * BY, value[:, half * nz:half * nz + nz], size1)
    wrap_hidden(size1)
    for i in range(steps):
        y0 = i * 2 * BY
        rows = slice(y0, y0 + 2 * BY)
        o = exact_dot(wout_ref[1], middle(1, y0, 0))
        for j in range(PX):
            keep = mask_ref[1, j, rows, :].astype(F32)
            r = j * 8
            phi, part = couple(1, keep, keep_ref[j, rows, :], o[r:r + 8], o[16 + r:24 + r])
            phi_ref[j, rows, :] = phi
            if send_ref is not None:
                send_ref[j, rows, :] = phi.astype(BF)
            total = total + part
    sum_ref[...] = jnp.broadcast_to(jnp.sum(total, axis=0, keepdims=True), (8, nz))


VMEM = pl.BlockSpec(memory_space=pltpu.VMEM)
SMEM = pl.BlockSpec(memory_space=pltpu.SMEM)


def prepare(enc_w, enc_b, in_w, hid_b, ctx_w, mid_w, mid_b, out_w):
    enc = jnp.transpose(enc_w, (1, 2, 3, 4, 0)).reshape(9, 3, CH)
    inw = jnp.transpose(in_w, (2, 3, 4, 5, 0, 1)).reshape(9, 3, LAYERS, CH)
    mid = jnp.transpose(mid_w, (0, 3, 4, 5, 1, 2)).reshape(LAYERS, 27, CH, CH)
    shapes = (
        (BY * HX0 * CH, 256), (BY * HX0 * CH, 256), (BY * (HX0 - 4) * CH, 256),
        (LAYERS, 256, 256), (LAYERS, BY * 2 * CH, 3 * 384), None, (LAYERS, 32, 256),
    )
    out_shape = [
        jax.ShapeDtypeStruct((LAYERS, CH, 128), F32) if s is None else jax.ShapeDtypeStruct(s, BF)
        for s in shapes
    ]
    return pl.pallas_call(
        prep_kernel,
        out_shape=out_shape,
        in_specs=[VMEM] * 8,
        out_specs=[VMEM] * 7,
        name="prep",
    )(enc, enc_b.reshape(1, CH), inw, hid_b, ctx_w, mid, mid_b, out_w)


def run_tick(tick, prevs, bases, masks, weights, out_b):
    lines, nz = masks.shape[2], masks.shape[3]
    last = tick == TICKS - 1

    def body(*refs):
        prev, rest = refs[:5], refs[5:]
        base, rest = rest[:5], rest[5:]
        mask, rest = rest[0], rest[1:]
        w, rest = rest[:7], rest[7:]
        out_b_ref, rest = rest[0], rest[1:]
        if last:
            phi, total = rest[:2]
            send, scratch = None, rest[2:]
        else:
            phi, send, total = rest[:3]
            scratch = rest[3:]
        tick_kernel(tick, lines, prev, base, mask, *w, out_b_ref, phi, send, total, *scratch)

    out_shape = [jax.ShapeDtypeStruct((PX, lines, nz), F32)]
    if not last:
        out_shape.append(jax.ShapeDtypeStruct((PX, lines, nz), BF))
    out_shape.append(jax.ShapeDtypeStruct((8, nz), F32))
    return pl.pallas_call(
        body,
        out_shape=out_shape,
        in_specs=[VMEM] * (5 + 5 + 1 + 7) + [SMEM],
        out_specs=[VMEM] * len(out_shape),
        scratch_shapes=[
            pltpu.VMEM((lines * GR, nz), F32),
            pltpu.VMEM(((lines + 2) * GR, nz), BF),
            pltpu.VMEM((lines, HX0 * CH, nz), BF),
            pltpu.VMEM((3, lines + 2, HX0 * CH, nz), BF),
            pltpu.VMEM((PX, lines, nz), F32),
        ],
        name=f"tick{tick}",
    )(*prevs, *bases, masks, *weights, out_b)


def shards(base, phi_prev, masks, enc_w, enc_b, in_w, ctx_w, hid_b, mid_w, mid_b, out_w, out_b):
    nt, ns = lax.axis_size("tm"), lax.axis_size("space")
    sites_total = masks.shape[1] * masks.shape[2] * masks.shape[3] * ns

    def moved(value, dt, ds):
        pairs = [
            (t * ns + s, (t + dt) % nt * ns + (s + ds) % ns) for t in range(nt) for s in range(ns)
        ]
        return lax.ppermute(value, ("tm", "space"), pairs)

    def around(value, dt):
        return [moved(value, dt, ds) if dt or ds else value for ds in (2, 1, 0, -1, -2)]

    start = base[:, 0]
    starts = around(start.astype(BF), 0)
    starts[2] = start
    prevs = around(phi_prev[0].astype(BF), 1)
    weights = prepare(enc_w, enc_b, in_w, hid_b, ctx_w, mid_w, mid_b, out_w)
    phi0, send, sum0 = run_tick(0, prevs, starts, masks, weights, out_b)
    phi1, sum1 = run_tick(1, around(send, 1), starts, masks, weights, out_b)
    total = jnp.stack([jnp.sum(sum0[0]), jnp.sum(sum1[0])])
    total = jnp.broadcast_to(total[:, None], (2, 128))
    step = 1
    while step < ns:
        pairs = [(s, s ^ step) for s in range(ns)]
        total = total + lax.ppermute(total, "space", pairs)
        step *= 2
    return (jnp.stack([phi0, phi1])[:, None], total[:, :1] / sites_total)


def solution(mesh):
    in_specs = (
        P(None, "tm", "space", None, None),
        P("tm", "space", None, None),
        P(None, "space", None, None),
        P(), P(), P(), P(), P(), P(), P(), P(), P(),
    )
    out_specs = (P(None, "tm", "space", None, None), P(None, "tm"))
    return jax.shard_map(shards, mesh=mesh, in_specs=in_specs, out_specs=out_specs, check_vma=False)
```
